32 devices in a mesh: row: 4 (over y, core), col: 4 (over z), lag: 2 (over x).
Axes of the slice: x: 2, y: 2, z: 4, core: 2. Of those that a mesh axis runs over, the one named last changes fastest.
Arguments:
- trajectories: bfloat16 [4096, 4096], P(('row', 'col'), 'lag'), may hold values from -6 to 6
- pair_live: int32 [4, 4], replicated, may hold values from 0 to 1, as said below
Outputs:
- gram: bfloat16 [4096, 4096], P(('row', 'lag'), 'col')
The draws below stay inside these ranges and needn't reach their ends.
Inputs may be any that keep to these rules, and one draw needn't show every extreme that they name: `pair_live`: Symmetric, with every diagonal entry 1.
All inputs are finite; a program needn't handle non-finite values.
Results may differ from the reference program's by a relative error of at most 0.0015.
Values may be sent and summed in bfloat16 or wider, within the bound.
A program may use at most 64 MiB of HBM per device.

```python
import math
import jax
import jax.numpy as jnp
from jax import lax

EMBED = 4096
TB = 1024
NB = 4
NT = 4096


def draw_trajectories(key, part):
    key_noise = jax.random.fold_in(key, 11)
    key_freq = jax.random.fold_in(key, 12)
    key_phase = jax.random.fold_in(key, 13)
    key_amp = jax.random.fold_in(key, 14)
    key_sigma = jax.random.fold_in(key, 15)
    noise = jnp.clip(jax.random.normal(key_noise, (NT, EMBED), jnp.float32), -4.0, 4.0)
    centre = 0.9
    spread = 0.75 * TB / EMBED
    freq = centre + spread * jax.random.uniform(key_freq, (NT,), jnp.float32, 0.0, 1.0)
    phase = jax.random.uniform(key_phase, (NT,), jnp.float32, -math.pi, math.pi)
    amp = jnp.exp(jax.random.uniform(key_amp, (NT,), jnp.float32, math.log(0.8), math.log(1.3)))
    sigma = jnp.exp(jax.random.uniform(key_sigma, (NT,), jnp.float32, math.log(0.3), math.log(0.6)))
    times = jnp.arange(EMBED, dtype=jnp.float32)
    wave = jnp.cos(freq[:, None] * times[None, :] + phase[:, None])
    values = amp[:, None] * wave + sigma[:, None] * noise
    return jnp.clip(values, -6.0, 6.0).astype(jnp.bfloat16)


def draw_pair_live(key, part):
    bits = jax.random.randint(jax.random.fold_in(key, 21), (NB, NB), 0, 2, jnp.int32)
    index = jnp.arange(NB, dtype=jnp.int32)
    upper = jnp.where(index[:, None] <= index[None, :], bits, bits.T)
    return jnp.where(index[:, None] == index[None, :], 1, upper).astype(jnp.int32)


def setup_inputs(seed: int = 0) -> dict:
    key_of = jax.random.split(jax.random.key(seed), 3)
    trajectories = draw_trajectories(jax.random.fold_in(key_of[2], 71), 0)
    pair_live = draw_pair_live(jax.random.fold_in(key_of[2], 71), 0)
    return {"trajectories": trajectories, "pair_live": pair_live}


def reference(trajectories, pair_live):
    floats = trajectories.astype(jnp.float32)
    norms = jnp.sum(floats * floats, axis=1)
    live_float = pair_live.astype(jnp.float32)

    def one_block(block_index):
        start = (block_index * TB).astype(jnp.int32)
        rows = lax.dynamic_slice_in_dim(trajectories, start, TB, 0)
        row_norm = lax.dynamic_slice_in_dim(norms, start, TB, 0)
        inner = jnp.dot(rows, trajectories.T, preferred_element_type=jnp.float32)
        dist = row_norm[:, None] + norms[None, :] - 2.0 * inner
        live_row = jnp.repeat(live_float[block_index], TB)
        return (jnp.exp(-2.0 * dist / EMBED) * live_row[None, :]).astype(jnp.bfloat16)

    blocks = lax.map(one_block, jnp.arange(NB, dtype=jnp.int32))
    return blocks.reshape(NT, NT)
```

```python
import functools

import jax
import jax.numpy as jnp
from jax import lax
from jax.experimental import pallas as pl
from jax.experimental.pallas import tpu as pltpu
from jax.sharding import PartitionSpec as P

MESH = pl.DeviceIdType.MESH
SPLIT = 2
SUB = 1
NT_DIMS = (((1,), (1,)), ((), ()))


def kernel(
    rows, cols, lags, split, samples,
    x_ref, live_ref, out_ref,
    rb, rn, cn, tile, got, turned, given,
    own_sem, z_send, z_recv, c_send, c_recv, t_send, t_recv, m_send, m_recv,
):
    r, c, l = lax.axis_index("row"), lax.axis_index("col"), lax.axis_index("lag")
    units = cols * split
    m = rb.shape[1]
    mine = units // lags
    bits = rows.bit_length() - 1
    node = lax.bitwise_xor(r, c)
    base = jnp.where(node == 0, 0, units)
    at_end = jnp.logical_or(c == 0, c == cols - 1)
    inside = jnp.logical_and(r > 0, r < rows - 1)
    lo = jnp.where(inside, 1, 0)
    hi = jnp.where(inside, cols - 2, cols - 1)
    computes = jnp.logical_not(jnp.logical_and(inside, at_end))
    mirrors = jnp.logical_not(jnp.logical_or(inside, at_end))

    own = pltpu.make_async_copy(
        x_ref, rb.at[pl.ds(c * split, split)], own_sem
    )
    own.start()

    barrier = pltpu.get_barrier_semaphore()
    for j in range(1, rows):
        pl.semaphore_signal(
            barrier, device_id={"row": lax.rem(r + j, rows)}, device_id_type=MESH
        )
    for j in range(1, lags):
        pl.semaphore_signal(
            barrier, device_id={"lag": lax.rem(l + j, lags)}, device_id_type=MESH
        )

    @pl.when(c > 0)
    def _():
        pl.semaphore_signal(barrier, device_id={"col": c - 1}, device_id_type=MESH)

    @pl.when(c < cols - 1)
    def _():
        pl.semaphore_signal(barrier, device_id={"col": c + 1}, device_id_type=MESH)

    paired = jnp.logical_or(mirrors, jnp.logical_not(computes))

    @pl.when(paired)
    def _():
        for o in range(lags):
            pl.semaphore_signal(
                barrier, device_id={"row": c, "col": r, "lag": o}, device_id_type=MESH
            )

    beside = jnp.where(at_end, 1, 2) + jnp.where(paired, lags, 0)
    pl.semaphore_wait(barrier, rows - 1 + lags - 1 + beside)
    own.wait()

    chunk = m // SUB

    def part(ref, u, h):
        return ref.at[u, pl.ds(h * chunk, chunk)]

    def along(side, u, h):
        to = jnp.clip(c + 1 - 2 * side, 0, cols - 1)
        return pltpu.make_async_remote_copy(
            part(rb, u, h), part(rb, u, h), z_send.at[side, u, h], z_recv.at[u, h],
            device_id={"col": to}, device_id_type=MESH,
        )

    def down(bit, u, h):
        return pltpu.make_async_remote_copy(
            part(rb, base + u, h), part(rb, units + u, h), c_send.at[bit, u, h], c_recv.at[u, h],
            device_id={"row": lax.bitwise_xor(r, 1 << bit)}, device_id_type=MESH,
        )

    def has_child(bit):
        return lax.rem(node, 2 << bit) == 0

    def across(i, j):
        owner = i // mine
        hop = lax.rem(owner - l + lags, lags)
        slot = jnp.maximum(hop - 1, 0)
        return pltpu.make_async_remote_copy(
            tile.at[i, j], got.at[slot, lax.rem(i, mine), j],
            t_send.at[i, j], t_recv.at[slot, lax.rem(i, mine), j],
            device_id={"lag": owner}, device_id_type=MESH,
        )

    def valid(side, d):
        k = c - d if side == 0 else c + d
        return jnp.logical_and(k >= 0, k < cols), k

    def goes_on(side):
        return c < hi if side == 0 else c > lo

    def last_unit():
        return jnp.where(2 * c < cols, cols - 1, 0) * split + split - 1

    def unit_at(q, side):
        d = q // split
        ok, k = valid(side, d)
        u = jnp.clip(k, 0, cols - 1) * split + q - d * split
        return ok, jnp.logical_and(ok, jnp.logical_or(d > 0, side == 0)), u

    def one_round(q, carry):
        d = q // split
        here = [unit_at(q, side) for side in range(2)]

        def unit(side):
            return here[side]

        def one_chunk(h, carry):
            for side in range(2):
                ok, first, u = unit(side)

                ok = jnp.logical_and(ok, jnp.logical_or(d == 0, computes))

                @pl.when(jnp.logical_and(ok, d > 0))
                def _():
                    along(side, u, h).wait_recv()

                @pl.when(jnp.logical_and(ok, goes_on(side)))
                def _():
                    along(side, u, h).start()

                @pl.when(jnp.logical_and(first, node == 0))
                def _():
                    for bit in reversed(range(bits)):
                        down(bit, u, h).start()

            for side in range(2):
                ok, first, u = unit(side)

                @pl.when(jnp.logical_and(first, node != 0))
                def _():
                    down(0, u, h).wait_recv()
                    for bit in reversed(range(bits)):

                        @pl.when(has_child(bit))
                        def _():
                            down(bit, u, h).start()

            return carry

        lax.fori_loop(0, SUB, one_chunk, 0)

        for side in range(2):
            ok, first, u = unit(side)

            @pl.when(jnp.logical_and(first, computes))
            def _():
                a = rb[u].astype(jnp.float32)
                rn[u] = jnp.broadcast_to(
                    jnp.sum(a * a, axis=1, keepdims=True), rn.shape[1:]
                )
                b = rb[base + u].astype(jnp.float32)
                n = jnp.broadcast_to(jnp.sum(b * b, axis=1, keepdims=True), (m, 128))
                cn[u] = n.T[:8]

        def one_tile(i, j, leaves):
            @pl.when((i // mine != l) == leaves)
            def _():
                inner = lax.dot_general(
                    rb[i], rb[base + j], NT_DIMS, preferred_element_type=jnp.float32
                )
                tile[i, j] = rn[i][:, :1] + cn[j][:1] - 2.0 * inner
                if leaves:
                    across(i, j).start()

        def pairs(leaves, p, carry):
            q2, side2 = p // 2, lax.rem(p, 2)
            d2 = q2 // split
            k = c + jnp.where(side2 == 0, -d2, d2)
            found = jnp.logical_and(k >= 0, k < cols)
            found = jnp.logical_and(found, jnp.logical_or(d2 > 0, side2 == 0))
            v = jnp.clip(k, 0, cols - 1) * split + q2 - d2 * split
            for side in range(2):
                _, first, u = unit(side)

                @pl.when(jnp.logical_and(first, found))
                def _():
                    one_tile(u, v, leaves)

                    @pl.when(q2 < q)
                    def _():
                        one_tile(v, u, leaves)

            return carry

        @pl.when(computes)
        def _():
            for leaves in (True, False):
                lax.fori_loop(0, 2 * q + 2, functools.partial(pairs, leaves), 0)

        return carry

    lax.fori_loop(0, units, one_round, 0)

    live = live_ref[r, c].astype(jnp.float32)
    end = last_unit()

    def mirror(kk, j):
        return pltpu.make_async_remote_copy(
            turned.at[kk, j],
            given.at[j % mine, l * mine + kk],
            m_send.at[kk, j], m_recv.at[j % mine, l * mine + kk],
            device_id={"row": c, "col": r, "lag": j // mine}, device_id_type=MESH,
        )

    def finish(last, kk, carry):
        i = l * mine + kk
        for j in range(units):
            comes_last = jnp.logical_or(i == end, j == end)

            @pl.when(comes_last == last)
            def _():
                total = tile[i, j]
                for o in range(lags - 1):
                    pltpu.make_async_remote_copy(
                        tile.at[i, j], got.at[o, kk, j], t_send.at[i, j],
                        t_recv.at[o, kk, j],
                        device_id={"lag": lax.rem(l + 1, lags)},
                        device_id_type=MESH,
                    ).wait_recv()
                    total = total + got[o, kk, j]
                gram = jnp.exp(-2.0 * total / samples) * live
                out_ref[pl.ds(kk * m, m), j * m : (j + 1) * m] = gram.astype(
                    out_ref.dtype
                )

                @pl.when(mirrors)
                def _():
                    turned[kk, j] = gram.T.astype(out_ref.dtype)
                    mirror(kk, j).start()

        return carry

    @pl.when(computes)
    def _():
        for last in (False, True):
            lax.fori_loop(0, mine, functools.partial(finish, last), 0)

    @pl.when(mirrors)
    def _():
        def sent(kk, carry):
            for j in range(units):
                mirror(kk, j).wait_send()
            return carry

        lax.fori_loop(0, mine, sent, 0)

    @pl.when(jnp.logical_not(computes))
    def _():
        def landed(kk, carry):
            for i in range(units):
                pltpu.make_async_remote_copy(
                    turned.at[0, 0],
                    given.at[kk, i],
                    m_send.at[0, 0], m_recv.at[kk, i],
                    device_id={"row": c, "col": r, "lag": i // mine},
                    device_id_type=MESH,
                ).wait_recv()
                out_ref[pl.ds(kk * m, m), i * m : (i + 1) * m] = given[kk, i]
            return carry

        lax.fori_loop(0, mine, landed, 0)

    def drain(u, carry):
        k = u // split
        for h in range(SUB):

            got_it = jnp.logical_or(k == c, computes)

            @pl.when(jnp.logical_and(got_it, jnp.logical_and(k <= c, goes_on(0))))
            def _():
                along(0, u, h).wait_send()

            @pl.when(jnp.logical_and(got_it, jnp.logical_and(k >= c, goes_on(1))))
            def _():
                along(1, u, h).wait_send()

            for bit in range(bits):

                @pl.when(has_child(bit))
                def _():
                    down(bit, u, h).wait_send()

        @pl.when(jnp.logical_and(u // mine != l, computes))
        def _():
            def each(j, carry):
                across(u, j).wait_send()
                return carry

            lax.fori_loop(0, units, each, 0)

        return carry

    lax.fori_loop(0, units, drain, 0)


def on_device(rows, cols, lags, trajectories, pair_live):
    held, width = trajectories.shape
    split = SPLIT if held % (SPLIT * 128) == 0 else 1
    m = held // split
    units = cols * split
    mine = units // lags
    bits = rows.bit_length() - 1
    dma = pltpu.SemaphoreType.DMA
    return pl.pallas_call(
        functools.partial(kernel, rows, cols, lags, split, width * lags),
        out_shape=jax.ShapeDtypeStruct((mine * m, units * m), jnp.bfloat16),
        in_specs=[
            pl.BlockSpec(memory_space=pl.ANY),
            pl.BlockSpec(memory_space=pltpu.SMEM),
        ],
        out_specs=pl.BlockSpec(memory_space=pltpu.VMEM),
        scratch_shapes=[
            pltpu.VMEM((2 * units, m, width), jnp.bfloat16),
            pltpu.VMEM((units, m, 128), jnp.float32),
            pltpu.VMEM((units, 8, m), jnp.float32),
            pltpu.VMEM((units, units, m, m), jnp.float32),
            pltpu.VMEM((lags - 1, mine, units, m, m), jnp.float32),
            pltpu.VMEM((mine, units, m, m), jnp.bfloat16),
            pltpu.VMEM((mine, units, m, m), jnp.bfloat16),
            dma,
            dma((2, units, SUB)),
            dma((units, SUB)),
            dma((bits, units, SUB)),
            dma((units, SUB)),
            dma((units, units)),
            dma((lags - 1, mine, units)),
            dma((mine, units)),
            dma((mine, units)),
        ],
        compiler_params=pltpu.CompilerParams(
            collective_id=0, has_side_effects=True, vmem_limit_bytes=60 * 2**20
        ),
    )(trajectories.reshape(split, m, width), pair_live)


def solution(mesh):
    size = mesh.shape
    return jax.shard_map(
        functools.partial(on_device, size["row"], size["col"], size["lag"]),
        mesh=mesh,
        in_specs=(P(("row", "col"), "lag"), P()),
        out_specs=P(("row", "lag"), "col"),
        check_vma=False,
    )
```

```python
import functools

import jax
import jax.numpy as jnp
from jax import lax
from jax.experimental import pallas as pl
from jax.experimental.pallas import tpu as pltpu
from jax.sharding import PartitionSpec as P

MESH = pl.DeviceIdType.MESH
SPLIT = 2
SUB = 2
BEHIND = 2
NT_DIMS = (((1,), (1,)), ((), ()))


def kernel(
    rows, cols, lags, split, samples,
    x_ref, live_ref, out_ref,
    rb, rn, cn, tile, got, turned, done,
    own_sem, z_send, z_recv, c_send, c_recv, t_send, t_recv, m_send, m_recv,
):
    r, c, l = lax.axis_index("row"), lax.axis_index("col"), lax.axis_index("lag")
    units = cols * split
    m = rb.shape[1]
    mine = units // lags
    bits = rows.bit_length() - 1
    node = lax.bitwise_xor(r, c)
    base = jnp.where(node == 0, 0, units)
    chunk = m // SUB

    at_end = jnp.logical_or(c == 0, c == cols - 1)
    inside = jnp.logical_and(r > 0, r < rows - 1)
    lo = jnp.where(inside, 1, 0)
    hi = jnp.where(inside, cols - 2, cols - 1)
    computes = jnp.logical_not(jnp.logical_and(inside, at_end))
    mirrors = jnp.logical_not(jnp.logical_or(inside, at_end))
    paired = jnp.logical_or(mirrors, jnp.logical_not(computes))

    def place(u, where):
        k = u // split
        e = u - k * split
        left, right = where, cols - 1 - where
        d = jnp.abs(k - where)
        both = jnp.logical_and(d <= left, d <= right)
        before = split * (1 + jnp.minimum(d - 1, left) + jnp.minimum(d - 1, right))
        far = before + jnp.where(both, 2 * e + jnp.where(k > where, 1, 0), e)
        return jnp.where(d == 0, e, far)

    def unit_of(p):
        left, right = c, cols - 1 - c
        near = jnp.minimum(left, right)
        p1 = jnp.maximum(p - split, 0)
        p2 = jnp.maximum(p1 - 2 * split * near, 0)
        close = p1 < 2 * split * near
        d1 = p1 // (2 * split)
        rest = p1 - d1 * (2 * split)
        e1 = rest // 2
        s1 = rest - 2 * e1
        d2 = p2 // split
        e2 = p2 - d2 * split
        s2 = jnp.where(left < right, 1, 0)
        d = jnp.where(close, d1 + 1, d2 + near + 1)
        e = jnp.where(close, e1, e2)
        s = jnp.where(close, s1, s2)
        k = jnp.where(s == 0, c - d, c + d)
        k = jnp.clip(k, 0, cols - 1)
        return jnp.where(p < split, c * split + p, k * split + e)

    def along(side, u, p, h, src=None):
        to = jnp.clip(c + 1 - 2 * side, 0, cols - 1)
        rows_of = pl.ds(h * chunk, chunk)
        return pltpu.make_async_remote_copy(
            rb.at[p, rows_of] if src is None else src.at[p, rows_of],
            rb.at[place(u, to), rows_of],
            z_send.at[side, u, h], z_recv.at[u, h],
            device_id={"col": to}, device_id_type=MESH,
        )

    def down(bit, p, h):
        rows_of = pl.ds(h * chunk, chunk)
        return pltpu.make_async_remote_copy(
            rb.at[base + p, rows_of], rb.at[units + p, rows_of],
            c_send.at[bit, p, h], c_recv.at[p, h],
            device_id={"row": lax.bitwise_xor(r, 1 << bit)}, device_id_type=MESH,
        )

    def has_child(bit):
        return lax.rem(node, 2 << bit) == 0

    def across(i, j):
        owner = i // mine
        hop = lax.rem(owner - l + lags, lags)
        slot = jnp.maximum(hop - 1, 0)
        return pltpu.make_async_remote_copy(
            tile.at[i, j], got.at[slot, lax.rem(i, mine), j],
            t_send.at[i, j], t_recv.at[slot, lax.rem(i, mine), j],
            device_id={"lag": owner}, device_id_type=MESH,
        )

    def mirror(kk, j):
        i = l * mine + kk
        return pltpu.make_async_remote_copy(
            turned.at[kk, j], done.at[lax.rem(j, mine), i],
            m_send.at[kk, j], m_recv.at[lax.rem(j, mine), i],
            device_id={"row": c, "col": r, "lag": j // mine}, device_id_type=MESH,
        )

    own = pltpu.make_async_copy(x_ref, rb.at[pl.ds(0, split)], own_sem)
    own.start()

    barrier = pltpu.get_barrier_semaphore()
    for j in range(1, rows):
        pl.semaphore_signal(
            barrier, device_id={"row": lax.rem(r + j, rows)}, device_id_type=MESH
        )
    for j in range(1, lags):
        pl.semaphore_signal(
            barrier, device_id={"lag": lax.rem(l + j, lags)}, device_id_type=MESH
        )

    @pl.when(c > 0)
    def _():
        pl.semaphore_signal(barrier, device_id={"col": c - 1}, device_id_type=MESH)

    @pl.when(c < cols - 1)
    def _():
        pl.semaphore_signal(barrier, device_id={"col": c + 1}, device_id_type=MESH)

    @pl.when(paired)
    def _():
        for o in range(lags):
            pl.semaphore_signal(
                barrier, device_id={"row": c, "col": r, "lag": o}, device_id_type=MESH
            )

    beside = jnp.where(at_end, 1, 2) + jnp.where(paired, lags, 0)
    pl.semaphore_wait(barrier, rows - 1 + lags - 1 + beside)

    def goes_on(side):
        return c < hi if side == 0 else c > lo

    for side in range(2):

        @pl.when(goes_on(side))
        def _():
            for e in range(split):
                for h in range(SUB):
                    along(side, c * split + e, e, h, x_ref).start()

    own.wait()
    live = live_ref[r, c].astype(jnp.float32)

    def keep(i, j, distance):
        tile[i, j] = distance

        @pl.when(i // mine != l)
        def _():
            across(i, j).start()

    def strips(n, un):
        def inner_of(a, b):
            return lax.dot_general(a, b, NT_DIMS, preferred_element_type=jnp.float32)

        def two(at):
            return rb[pl.ds(at, 2)].reshape(2 * m, rb.shape[2])

        def row_pair(t, carry):
            inner = inner_of(rb[n], two(base + 2 * t))
            for o in range(2):
                j = 2 * t + o
                keep(
                    un, unit_of(j),
                    rn[n][:, :1] + cn[j][:1] - 2.0 * inner[:, o * m : (o + 1) * m],
                )
            return carry

        def column_pair(t, carry):
            inner = inner_of(two(2 * t), rb[base + n])
            for o in range(2):
                i = 2 * t + o
                keep(
                    unit_of(i), un,
                    rn[i][:, :1] + cn[n][:1] - 2.0 * inner[o * m : (o + 1) * m],
                )
            return carry

        def single(i, j):
            inner = inner_of(rb[i], rb[base + j])
            keep(unit_of(i), unit_of(j), rn[i][:, :1] + cn[j][:1] - 2.0 * inner)

        odd = lax.rem(n, 2)
        lax.fori_loop(0, (n + 1) // 2, row_pair, 0)

        def last_one(t, carry):
            single(n - odd, n)
            return carry

        lax.fori_loop(0, 1, last_one, 0)
        lax.fori_loop(0, n // 2, column_pair, 0)

    def finish(n, un):
        def close(i, j):
            kk = lax.rem(i, mine)
            total = tile[i, j]
            for o in range(lags - 1):
                pltpu.make_async_remote_copy(
                    tile.at[i, j], got.at[o, kk, j], t_send.at[i, j],
                    t_recv.at[o, kk, j],
                    device_id={"lag": lax.rem(l + 1, lags)},
                    device_id_type=MESH,
                ).wait_recv()
                total = total + got[o, kk, j]
            gram = jnp.exp(-2.0 * total / samples) * live
            done[kk, j] = gram.astype(done.dtype)

            @pl.when(mirrors)
            def _():
                turned[kk, j] = gram.T.astype(turned.dtype)
                mirror(kk, j).start()

        def one(t, carry):
            ut = unit_of(jnp.minimum(t, 2 * n - t))
            i = jnp.where(t <= n, un, ut)
            j = jnp.where(t <= n, ut, un)

            @pl.when(i // mine == l)
            def _():
                close(i, j)

            return carry

        lax.fori_loop(0, 2 * n + 1, one, 0)

    def step(n, carry):
        u = unit_of(n)
        k = u // split

        @pl.when(jnp.logical_and(n >= split, computes))
        def _():
            for h in range(SUB):
                along(0, u, n, h).wait_recv()
                for side in range(2):
                    onward = k < c if side == 0 else k > c

                    @pl.when(jnp.logical_and(onward, goes_on(side)))
                    def _():
                        along(side, u, n, h).start()

                @pl.when(node == 0)
                def _():
                    for bit in reversed(range(bits)):
                        down(bit, n, h).start()

        @pl.when(jnp.logical_and(n < split, node == 0))
        def _():
            for h in range(SUB):
                for bit in reversed(range(bits)):
                    down(bit, n, h).start()

        @pl.when(node != 0)
        def _():
            for h in range(SUB):
                down(0, n, h).wait_recv()
                for bit in reversed(range(bits)):

                    @pl.when(has_child(bit))
                    def _():
                        down(bit, n, h).start()

        @pl.when(computes)
        def _():
            a = rb[n].astype(jnp.float32)
            rn[n] = jnp.broadcast_to(
                jnp.sum(a * a, axis=1, keepdims=True), rn.shape[1:]
            )
            b = rb[base + n].astype(jnp.float32)
            s = jnp.broadcast_to(jnp.sum(b * b, axis=1, keepdims=True), (m, 128))
            cn[n] = s.T[:8]
            strips(n, u)

            @pl.when(n >= BEHIND)
            def _():
                finish(n - BEHIND, unit_of(n - BEHIND))

        return carry

    lax.fori_loop(0, units, step, 0)

    @pl.when(computes)
    def _():
        def tail(n, carry):
            finish(n, unit_of(n))
            return carry

        lax.fori_loop(units - BEHIND, units, tail, 0)

    @pl.when(jnp.logical_not(computes))
    def _():
        def landed(t, carry):
            kk, i = t // units, lax.rem(t, units)
            pltpu.make_async_remote_copy(
                turned.at[0, 0], done.at[kk, i], m_send.at[0, 0], m_recv.at[kk, i],
                device_id={"row": c, "col": r, "lag": i // mine}, device_id_type=MESH,
            ).wait_recv()
            return carry

        lax.fori_loop(0, mine * units, landed, 0)

    def lay(kk, carry):
        for j in range(units):
            out_ref[pl.ds(kk * m, m), j * m : (j + 1) * m] = done[kk, j]
        return carry

    lax.fori_loop(0, mine, lay, 0)

    def drain(p, carry):
        u = unit_of(p)
        k = u // split
        got_it = jnp.logical_or(k == c, computes)
        for h in range(SUB):

            @pl.when(jnp.logical_and(got_it, jnp.logical_and(k <= c, goes_on(0))))
            def _():
                along(0, u, p, h).wait_send()

            @pl.when(jnp.logical_and(got_it, jnp.logical_and(k >= c, goes_on(1))))
            def _():
                along(1, u, p, h).wait_send()

            for bit in range(bits):

                @pl.when(has_child(bit))
                def _():
                    down(bit, p, h).wait_send()

        @pl.when(jnp.logical_and(u // mine != l, computes))
        def _():
            def each(j, carry):
                across(u, j).wait_send()
                return carry

            lax.fori_loop(0, units, each, 0)

        return carry

    lax.fori_loop(0, units, drain, 0)

    @pl.when(mirrors)
    def _():
        def sent(t, carry):
            mirror(t // units, lax.rem(t, units)).wait_send()
            return carry

        lax.fori_loop(0, mine * units, sent, 0)


def on_device(rows, cols, lags, trajectories, pair_live):
    held, width = trajectories.shape
    split = SPLIT if held % (SPLIT * 128) == 0 else 1
    m = held // split
    units = cols * split
    mine = units // lags
    bits = rows.bit_length() - 1
    dma = pltpu.SemaphoreType.DMA
    return pl.pallas_call(
        functools.partial(kernel, rows, cols, lags, split, width * lags),
        out_shape=jax.ShapeDtypeStruct((mine * m, units * m), jnp.bfloat16),
        in_specs=[
            pl.BlockSpec(memory_space=pl.ANY),
            pl.BlockSpec(memory_space=pltpu.SMEM),
        ],
        out_specs=pl.BlockSpec(memory_space=pltpu.VMEM),
        scratch_shapes=[
            pltpu.VMEM((2 * units, m, width), jnp.bfloat16),
            pltpu.VMEM((units, m, 128), jnp.float32),
            pltpu.VMEM((units, 8, m), jnp.float32),
            pltpu.VMEM((units, units, m, m), jnp.float32),
            pltpu.VMEM((lags - 1, mine, units, m, m), jnp.float32),
            pltpu.VMEM((mine, units, m, m), jnp.bfloat16),
            pltpu.VMEM((mine, units, m, m), jnp.bfloat16),
            dma,
            dma((2, units, SUB)),
            dma((units, SUB)),
            dma((bits, units, SUB)),
            dma((units, SUB)),
            dma((units, units)),
            dma((lags - 1, mine, units)),
            dma((mine, units)),
            dma((mine, units)),
        ],
        compiler_params=pltpu.CompilerParams(
            collective_id=0, has_side_effects=True, vmem_limit_bytes=60 * 2**20
        ),
    )(trajectories.reshape(split, m, width), pair_live)


def solution(mesh):
    size = mesh.shape
    return jax.shard_map(
        functools.partial(on_device, size["row"], size["col"], size["lag"]),
        mesh=mesh,
        in_specs=(P(("row", "col"), "lag"), P()),
        out_specs=P(("row", "lag"), "col"),
        check_vma=False,
    )
```

```python
import functools

import jax
import jax.numpy as jnp
from jax import lax
from jax.experimental import pallas as pl
from jax.experimental.pallas import tpu as pltpu
from jax.sharding import PartitionSpec as P

MESH = pl.DeviceIdType.MESH
SPLIT = 2
SUB = 2
BEHIND = 3
NT_DIMS = (((1,), (1,)), ((), ()))


def kernel(
    rows, cols, lags, split, samples,
    x_ref, live_ref, out_ref,
    rb, rn, cn, tile, got, turned, done,
    own_sem, z_send, z_recv, c_send, c_recv, t_send, t_recv, m_send, m_recv,
):
    r, c, l = lax.axis_index("row"), lax.axis_index("col"), lax.axis_index("lag")
    units = cols * split
    m = rb.shape[1]
    mine = units // lags
    bits = rows.bit_length() - 1
    node = lax.bitwise_xor(r, c)
    base = jnp.where(node == 0, 0, units)
    chunk = m // SUB

    at_end = jnp.logical_or(c == 0, c == cols - 1)
    inside = jnp.logical_and(r > 0, r < rows - 1)
    lo = jnp.where(inside, 1, 0)
    hi = jnp.where(inside, cols - 2, cols - 1)
    computes = jnp.logical_not(jnp.logical_and(inside, at_end))
    mirrors = jnp.logical_not(jnp.logical_or(inside, at_end))
    paired = jnp.logical_or(mirrors, jnp.logical_not(computes))

    def place(u, where):
        k = lax.div(u, split)
        e = u - k * split
        left, right = where, cols - 1 - where
        d = jnp.abs(k - where)
        both = jnp.logical_and(d <= left, d <= right)
        before = split * (1 + jnp.minimum(d - 1, left) + jnp.minimum(d - 1, right))
        second = (k > where) != (left < right)
        far = before + jnp.where(both, 2 * e + jnp.where(second, 1, 0), e)
        return jnp.where(d == 0, e, far)

    def unit_of(p):
        left, right = c, cols - 1 - c
        near = jnp.minimum(left, right)
        p1 = jnp.maximum(p - split, 0)
        p2 = jnp.maximum(p1 - 2 * split * near, 0)
        close = p1 < 2 * split * near
        d1 = p1 // (2 * split)
        rest = p1 - d1 * (2 * split)
        e1 = rest // 2
        s1 = jnp.where(left < right, 1 - rest + 2 * e1, rest - 2 * e1)
        d2 = p2 // split
        e2 = p2 - d2 * split
        s2 = jnp.where(left < right, 1, 0)
        d = jnp.where(close, d1 + 1, d2 + near + 1)
        e = jnp.where(close, e1, e2)
        s = jnp.where(close, s1, s2)
        k = jnp.where(s == 0, c - d, c + d)
        k = jnp.clip(k, 0, cols - 1)
        return jnp.where(p < split, c * split + p, k * split + e)

    def along(side, u, p, h, src=None):
        to = jnp.clip(c + 1 - 2 * side, 0, cols - 1)
        rows_of = pl.ds(h * chunk, chunk)
        return pltpu.make_async_remote_copy(
            rb.at[p, rows_of] if src is None else src.at[p, rows_of],
            rb.at[place(u, to), rows_of],
            z_send.at[side, u, h], z_recv.at[u, h],
            device_id={"col": to}, device_id_type=MESH,
        )

    def down(bit, p, h):
        rows_of = pl.ds(h * chunk, chunk)
        return pltpu.make_async_remote_copy(
            rb.at[base + p, rows_of], rb.at[units + p, rows_of],
            c_send.at[bit, p, h], c_recv.at[p, h],
            device_id={"row": lax.bitwise_xor(r, 1 << bit)}, device_id_type=MESH,
        )

    def has_child(bit):
        return lax.rem(node, 2 << bit) == 0

    def across(i, j):
        owner = lax.div(i, mine)
        hop = lax.rem(owner - l + lags, lags)
        slot = jnp.maximum(hop - 1, 0)
        return pltpu.make_async_remote_copy(
            tile.at[i, j], got.at[slot, lax.rem(i, mine), j],
            t_send.at[i, j], t_recv.at[slot, lax.rem(i, mine), j],
            device_id={"lag": owner}, device_id_type=MESH,
        )

    def mirror(kk, j):
        i = l * mine + kk
        return pltpu.make_async_remote_copy(
            turned.at[kk, j], done.at[lax.rem(j, mine), i],
            m_send.at[kk, j], m_recv.at[lax.rem(j, mine), i],
            device_id={"row": c, "col": r, "lag": lax.div(j, mine)}, device_id_type=MESH,
        )

    at = [unit_of(jnp.int32(p)) for p in range(units)]

    def order(p):
        u = at[-1]
        for i in range(units - 1):
            u = jnp.where(p == i, at[i], u)
        return u

    own = pltpu.make_async_copy(x_ref, rb.at[pl.ds(0, split)], own_sem)
    own.start()

    barrier = pltpu.get_barrier_semaphore()
    for j in range(1, rows):
        pl.semaphore_signal(
            barrier, device_id={"row": lax.rem(r + j, rows)}, device_id_type=MESH
        )
    for j in range(1, lags):
        pl.semaphore_signal(
            barrier, device_id={"lag": lax.rem(l + j, lags)}, device_id_type=MESH
        )

    @pl.when(c > 0)
    def _():
        pl.semaphore_signal(barrier, device_id={"col": c - 1}, device_id_type=MESH)

    @pl.when(c < cols - 1)
    def _():
        pl.semaphore_signal(barrier, device_id={"col": c + 1}, device_id_type=MESH)

    @pl.when(paired)
    def _():
        for o in range(lags):
            pl.semaphore_signal(
                barrier, device_id={"row": c, "col": r, "lag": o}, device_id_type=MESH
            )

    beside = jnp.where(at_end, 1, 2) + jnp.where(paired, lags, 0)
    pl.semaphore_wait(barrier, rows - 1 + lags - 1 + beside)

    def goes_on(side):
        return c < hi if side == 0 else c > lo

    for side in range(2):

        @pl.when(goes_on(side))
        def _():
            for e in range(split):
                for h in range(SUB):
                    along(side, c * split + e, e, h, x_ref).start()

    own.wait()
    live = live_ref[r, c].astype(jnp.float32)

    def inner_of(a, b):
        return lax.dot_general(a, b, NT_DIMS, preferred_element_type=jnp.float32)

    def two(at):
        return rb[pl.ds(at, 2)].reshape(2 * m, rb.shape[2])

    def keep(p, q, inner, held=False):
        i, j = order(p), order(q)
        tile[i, j] = rn[p][:, :1] + cn[q][:1] - 2.0 * inner

        @pl.when(jnp.logical_and(lax.div(i, mine) != l, jnp.logical_not(held)))
        def _():
            across(i, j).start()

    def holds(n):
        return jnp.logical_and(n == units - 2, inside)

    def release(n):
        i = order(n)

        @pl.when(lax.div(i, mine) != l)
        def _():
            loop(n, lambda q: across(i, order(q)).start())

    def wide(n, t):
        inner = inner_of(rb[n], two(base + 2 * t))
        for j in range(2):
            keep(n, 2 * t + j, inner[:, j * m : (j + 1) * m], holds(n))

    def tall(s, n):
        inner = inner_of(two(2 * s), rb[base + n])
        for i in range(2):
            keep(2 * s + i, n, inner[i * m : (i + 1) * m])

    def loop(count, body):
        def one(t, carry):
            body(t)
            return carry

        lax.fori_loop(0, count, one, 0)

    def close(p, q, sends):
        i, j = order(p), order(q)
        kk = lax.rem(i, mine)
        total = tile[i, j]
        for o in range(lags - 1):
            pltpu.make_async_remote_copy(
                tile.at[i, j], got.at[o, kk, j], t_send.at[i, j], t_recv.at[o, kk, j],
                device_id={"lag": lax.rem(l + 1, lags)}, device_id_type=MESH,
            ).wait_recv()
            total = total + got[o, kk, j]
        gram = jnp.exp(-2.0 * total / samples) * live
        done[kk, j] = gram.astype(done.dtype)

        @pl.when(mirrors)
        def _():
            turned[kk, j] = gram.T.astype(turned.dtype)

            @pl.when(sends)
            def _():
                mirror(kk, j).start()

    def finish(n, sends):
        def one(p, q):
            @pl.when(lax.div(order(p), mine) == l)
            def _():
                close(p, q, sends)

        @pl.when(lax.div(order(n), mine) == l)
        def _():
            loop(n + 1, lambda q: close(n, q, sends))

        loop(n, lambda p: one(p, n))

    early = units - 2 - BEHIND
    near = jnp.abs(c - r) < 2

    def send_mirrored(p):
        i = order(p)

        @pl.when(lax.div(i, mine) == l)
        def _():
            loop(early, lambda q: mirror(lax.rem(i, mine), order(q)).start())

    def gather_rows(n):
        u = order(n)
        k = lax.div(u, split)
        for h in range(SUB):

            @pl.when(jnp.logical_and(n >= split, computes))
            def _():
                along(0, u, n, h).wait_recv()
                for side in range(2):
                    onward = k < c if side == 0 else k > c

                    @pl.when(jnp.logical_and(onward, goes_on(side)))
                    def _():
                        along(side, u, n, h).start()

            @pl.when(node == 0)
            def _():
                for bit in reversed(range(bits)):
                    down(bit, n, h).start()

    def gather_columns(n):
        @pl.when(node != 0)
        def _():
            for h in range(SUB):
                down(0, n, h).wait_recv()
                for bit in reversed(range(bits)):

                    @pl.when(has_child(bit))
                    def _():
                        down(bit, n, h).start()

    def row_norms(n):
        a = rb[n].astype(jnp.float32)
        rn[n] = jnp.broadcast_to(jnp.sum(a * a, axis=1, keepdims=True), rn.shape[1:])

    def column_norms(n):
        b = rb[base + n].astype(jnp.float32)
        s = jnp.broadcast_to(jnp.sum(b * b, axis=1, keepdims=True), (m, 128))
        cn[n] = s.T[:8]

    def step(n):
        odd = lax.rem(n, 2)
        gather_rows(n)

        @pl.when(computes)
        def _():
            row_norms(n)
            loop(lax.div(n, 2), lambda t: wide(n, t))

            @pl.when(odd == 1)
            def _():
                keep(n, n - 1, inner_of(rb[n], rb[base + n - 1]), holds(n))

            @pl.when(holds(n - 1))
            def _():
                release(n - 1)

        gather_columns(n)

        @pl.when(computes)
        def _():
            column_norms(n)
            loop(lax.div(n + 1, 2), lambda t: tall(t, n))

            @pl.when(odd == 0)
            def _():
                keep(n, n, inner_of(rb[n], rb[base + n]))

            @pl.when(n >= BEHIND)
            def _():
                @pl.when(jnp.logical_and(n == units - 2, jnp.logical_and(mirrors, jnp.logical_not(near))))
                def _():
                    loop(early, send_mirrored)

                finish(n - BEHIND, jnp.logical_or(near, n >= units - 2))

    loop(units, step)

    @pl.when(computes)
    def _():
        loop(BEHIND, lambda o: finish(units - BEHIND + o, True))

    @pl.when(jnp.logical_not(computes))
    def _():
        def landed(t, carry):
            kk, i = t // units, lax.rem(t, units)
            pltpu.make_async_remote_copy(
                turned.at[0, 0], done.at[kk, i], m_send.at[0, 0], m_recv.at[kk, i],
                device_id={"row": c, "col": r, "lag": i // mine}, device_id_type=MESH,
            ).wait_recv()
            return carry

        lax.fori_loop(0, mine * units, landed, 0)

    def lay(kk, carry):
        for j in range(units):
            out_ref[pl.ds(kk * m, m), j * m : (j + 1) * m] = done[kk, j]
        return carry

    lax.fori_loop(0, mine, lay, 0)

    def drain(p, carry):
        u = order(p)
        k = lax.div(u, split)
        got_it = jnp.logical_or(k == c, computes)
        for h in range(SUB):

            @pl.when(jnp.logical_and(got_it, jnp.logical_and(k <= c, goes_on(0))))
            def _():
                along(0, u, p, h).wait_send()

            @pl.when(jnp.logical_and(got_it, jnp.logical_and(k >= c, goes_on(1))))
            def _():
                along(1, u, p, h).wait_send()

            for bit in range(bits):

                @pl.when(has_child(bit))
                def _():
                    down(bit, p, h).wait_send()

        @pl.when(jnp.logical_and(lax.div(u, mine) != l, computes))
        def _():
            def each(j, carry):
                across(u, j).wait_send()
                return carry

            lax.fori_loop(0, units, each, 0)

        return carry

    lax.fori_loop(0, units, drain, 0)

    @pl.when(mirrors)
    def _():
        def sent(t, carry):
            mirror(t // units, lax.rem(t, units)).wait_send()
            return carry

        lax.fori_loop(0, mine * units, sent, 0)


def on_device(rows, cols, lags, trajectories, pair_live):
    held, width = trajectories.shape
    split = SPLIT if held % (SPLIT * 128) == 0 else 1
    m = held // split
    units = cols * split
    mine = units // lags
    bits = rows.bit_length() - 1
    dma = pltpu.SemaphoreType.DMA
    return pl.pallas_call(
        functools.partial(kernel, rows, cols, lags, split, width * lags),
        out_shape=jax.ShapeDtypeStruct((mine * m, units * m), jnp.bfloat16),
        in_specs=[
            pl.BlockSpec(memory_space=pl.ANY),
            pl.BlockSpec(memory_space=pltpu.SMEM),
        ],
        out_specs=pl.BlockSpec(memory_space=pltpu.VMEM),
        scratch_shapes=[
            pltpu.VMEM((2 * units, m, width), jnp.bfloat16),
            pltpu.VMEM((units, m, 128), jnp.float32),
            pltpu.VMEM((units, 8, m), jnp.float32),
            pltpu.VMEM((units, units, m, m), jnp.float32),
            pltpu.VMEM((lags - 1, mine, units, m, m), jnp.float32),
            pltpu.VMEM((mine, units, m, m), jnp.bfloat16),
            pltpu.VMEM((mine, units, m, m), jnp.bfloat16),
            dma,
            dma((2, units, SUB)),
            dma((units, SUB)),
            dma((bits, units, SUB)),
            dma((units, SUB)),
            dma((units, units)),
            dma((lags - 1, mine, units)),
            dma((mine, units)),
            dma((mine, units)),
        ],
        compiler_params=pltpu.CompilerParams(
            collective_id=0, has_side_effects=True, vmem_limit_bytes=60 * 2**20
        ),
    )(trajectories.reshape(split, m, width), pair_live)


def solution(mesh):
    size = mesh.shape
    return jax.shard_map(
        functools.partial(on_device, size["row"], size["col"], size["lag"]),
        mesh=mesh,
        in_specs=(P(("row", "col"), "lag"), P()),
        out_specs=P(("row", "lag"), "col"),
        check_vma=False,
    )
```

```python
import functools

import jax
import jax.numpy as jnp
from jax import lax
from jax.experimental import pallas as pl
from jax.experimental.pallas import tpu as pltpu
from jax.sharding import PartitionSpec as P

MESH = pl.DeviceIdType.MESH
SPLIT = 2
SUB = 2
BEHIND = 2
NT_DIMS = (((1,), (1,)), ((), ()))


def kernel(
    rows, cols, lags, split, samples,
    x_ref, live_ref, result,
    out_ref, out_sem, rb, rn, cn, tile, got, turned, done,
    own_sem, z_send, z_recv, c_send, c_recv, t_send, t_recv, m_send, m_recv,
):
    r, c, l = lax.axis_index("row"), lax.axis_index("col"), lax.axis_index("lag")
    units = cols * split
    m = rb.shape[1]
    mine = units // lags
    bits = rows.bit_length() - 1
    node = lax.bitwise_xor(r, c)
    base = jnp.where(node == 0, 0, units)
    chunk = m // SUB

    at_end = jnp.logical_or(c == 0, c == cols - 1)
    inside = jnp.logical_and(r > 0, r < rows - 1)
    partial = jnp.logical_and(inside, at_end)
    limit = jnp.where(partial, mine, units)
    mirrors = jnp.logical_not(jnp.logical_or(inside, at_end))
    on_diagonal = r == c
    turns = jnp.logical_and(on_diagonal, jnp.logical_not(at_end))
    swaps = jnp.logical_and(inside, jnp.logical_not(jnp.logical_or(at_end, on_diagonal)))
    paired = jnp.logical_not(jnp.logical_or(on_diagonal, jnp.logical_and(at_end, jnp.logical_not(partial))))

    first = jnp.where(on_diagonal, 2 * c < cols, c < r)
    early = jnp.where(first, 0, lags - 1)
    late = lags - 1 - early

    def near_lag(end):
        return jnp.where(end == 0, 0, lags - 1)

    def gives(a, b):
        given = jnp.logical_and(mirrors, b != near_lag(r))
        if lags == 1:
            return given
        swap = jnp.logical_and(swaps, jnp.logical_and(a == early, b == early))
        turn = jnp.logical_and(turns, jnp.logical_and(a == early, b != early))
        return jnp.logical_or(given, jnp.logical_or(swap, turn))

    def takes(a, b):
        taken = jnp.logical_and(partial, a != near_lag(c))
        if lags == 1:
            return taken
        swap = jnp.logical_and(swaps, jnp.logical_and(a == late, b == late))
        turn = jnp.logical_and(turns, jnp.logical_and(a != early, b == early))
        return jnp.logical_or(taken, jnp.logical_or(swap, turn))

    def double(p, q, a, b):
        return jnp.logical_and(on_diagonal, jnp.logical_and(a == b, p < q))

    def sent(p, q):
        a, b = lax.div(order(p), mine), lax.div(order(q), mine)
        skipped = jnp.logical_or(takes(a, b), double(p, q, a, b))
        return jnp.logical_and(a != l, jnp.logical_not(skipped))

    def closed(p, q):
        a, b = lax.div(order(p), mine), lax.div(order(q), mine)
        skipped = jnp.logical_or(takes(a, b), double(p, q, a, b))
        return jnp.logical_and(a == l, jnp.logical_not(skipped))

    def place(u, where):
        k = lax.div(u, split)
        e = u - k * split
        left, right = where, cols - 1 - where
        d = jnp.abs(k - where)
        both = jnp.logical_and(d <= left, d <= right)
        before = split * (1 + jnp.minimum(d - 1, left) + jnp.minimum(d - 1, right))
        second = (k > where) != (left < right)
        far = before + jnp.where(both, 2 * e + jnp.where(second, 1, 0), e)
        return jnp.where(d == 0, e, far)

    def unit_of(p):
        left, right = c, cols - 1 - c
        near = jnp.minimum(left, right)
        p1 = jnp.maximum(p - split, 0)
        p2 = jnp.maximum(p1 - 2 * split * near, 0)
        close = p1 < 2 * split * near
        d1 = p1 // (2 * split)
        rest = p1 - d1 * (2 * split)
        e1 = rest // 2
        s1 = jnp.where(left < right, 1 - rest + 2 * e1, rest - 2 * e1)
        d2 = p2 // split
        e2 = p2 - d2 * split
        s2 = jnp.where(left < right, 1, 0)
        d = jnp.where(close, d1 + 1, d2 + near + 1)
        e = jnp.where(close, e1, e2)
        s = jnp.where(close, s1, s2)
        k = jnp.where(s == 0, c - d, c + d)
        k = jnp.clip(k, 0, cols - 1)
        return jnp.where(p < split, c * split + p, k * split + e)

    def along(side, u, p, h, src=None):
        to = jnp.clip(c + 1 - 2 * side, 0, cols - 1)
        rows_of = pl.ds(h * chunk, chunk)
        return pltpu.make_async_remote_copy(
            rb.at[p, rows_of] if src is None else src.at[p, rows_of],
            rb.at[place(u, to), rows_of],
            z_send.at[side, u, h], z_recv.at[u, h],
            device_id={"col": to}, device_id_type=MESH,
        )

    def down(bit, p, h):
        rows_of = pl.ds(h * chunk, chunk)
        return pltpu.make_async_remote_copy(
            rb.at[base + p, rows_of], rb.at[units + p, rows_of],
            c_send.at[bit, p, h], c_recv.at[p, h],
            device_id={"row": lax.bitwise_xor(r, 1 << bit)}, device_id_type=MESH,
        )

    def has_child(bit):
        return lax.rem(node, 2 << bit) == 0

    def across(i, j):
        owner = lax.div(i, mine)
        hop = lax.rem(owner - l + lags, lags)
        slot = jnp.maximum(hop - 1, 0)
        return pltpu.make_async_remote_copy(
            tile.at[i, j], got.at[slot, lax.rem(i, mine), j],
            t_send.at[i, j], t_recv.at[slot, lax.rem(i, mine), j],
            device_id={"lag": owner}, device_id_type=MESH,
        )

    def mirror(kk, j):
        i = l * mine + kk
        return pltpu.make_async_remote_copy(
            turned.at[kk, j], done.at[lax.rem(j, mine), i],
            m_send.at[kk, j], m_recv.at[lax.rem(j, mine), i],
            device_id={"row": c, "col": r, "lag": lax.div(j, mine)}, device_id_type=MESH,
        )

    at = [unit_of(jnp.int32(p)) for p in range(units)]

    def order(p):
        u = at[-1]
        for i in range(units - 1):
            u = jnp.where(p == i, at[i], u)
        return u

    own = pltpu.make_async_copy(x_ref, rb.at[pl.ds(0, split)], own_sem)
    own.start()

    barrier = pltpu.get_barrier_semaphore()
    for j in range(1, rows):
        pl.semaphore_signal(
            barrier, device_id={"row": lax.rem(r + j, rows)}, device_id_type=MESH
        )
    for j in range(1, lags):
        pl.semaphore_signal(
            barrier, device_id={"lag": lax.rem(l + j, lags)}, device_id_type=MESH
        )

    @pl.when(c > 0)
    def _():
        pl.semaphore_signal(barrier, device_id={"col": c - 1}, device_id_type=MESH)

    @pl.when(c < cols - 1)
    def _():
        pl.semaphore_signal(barrier, device_id={"col": c + 1}, device_id_type=MESH)

    @pl.when(paired)
    def _():
        for o in range(lags):
            pl.semaphore_signal(
                barrier, device_id={"row": c, "col": r, "lag": o}, device_id_type=MESH
            )

    beside = jnp.where(at_end, 1, 2) + jnp.where(paired, lags, 0)
    pl.semaphore_wait(barrier, rows - 1 + lags - 1 + beside)

    def goes_on(side, u):
        a = lax.div(u, mine)
        if side == 0:
            return c < jnp.where(jnp.logical_and(inside, a != lags - 1), cols - 2, cols - 1)
        return c > jnp.where(jnp.logical_and(inside, a != 0), 1, 0)

    for side in range(2):
        for e in range(split):

            @pl.when(goes_on(side, c * split + e))
            def _():
                for h in range(SUB):
                    along(side, c * split + e, e, h, x_ref).start()

    own.wait()
    live = live_ref[r, c].astype(jnp.float32)

    def inner_of(a, b):
        return lax.dot_general(a, b, NT_DIMS, preferred_element_type=jnp.float32)

    def two(at):
        return rb[pl.ds(at, 2)].reshape(2 * m, rb.shape[2])

    def keep(p, q, inner, held=False):
        i, j = order(p), order(q)
        tile[i, j] = rn[p][:, :1] + cn[q][:1] - 2.0 * inner

        @pl.when(jnp.logical_and(sent(p, q), jnp.logical_not(held)))
        def _():
            across(i, j).start()

    def holds(n):
        return jnp.logical_and(n == units - 2, inside)

    def release(n):
        i = order(n)

        def one(q):
            @pl.when(sent(n, q))
            def _():
                across(i, order(q)).start()

        loop(n, one)

    def wide(n, t):
        inner = inner_of(rb[n], two(base + 2 * t))
        for j in range(2):
            keep(n, 2 * t + j, inner[:, j * m : (j + 1) * m], holds(n))

    def tall(s, n):
        inner = inner_of(two(2 * s), rb[base + n])
        for i in range(2):
            keep(2 * s + i, n, inner[i * m : (i + 1) * m])

    def loop(count, body):
        def one(t, carry):
            body(t)
            return carry

        lax.fori_loop(0, count, one, 0)

    def close(p, q, sends):
        i, j = order(p), order(q)
        kk = lax.rem(i, mine)
        total = tile[i, j]
        for o in range(lags - 1):
            pltpu.make_async_remote_copy(
                tile.at[i, j], got.at[o, kk, j], t_send.at[i, j], t_recv.at[o, kk, j],
                device_id={"lag": lax.rem(l + 1, lags)}, device_id_type=MESH,
            ).wait_recv()
            total = total + got[o, kk, j]
        gram = jnp.exp(-2.0 * total / samples) * live
        done[kk, j] = gram.astype(done.dtype)

        @pl.when(double(q, p, lax.div(i, mine), lax.div(j, mine)))
        def _():
            done[lax.rem(j, mine), i] = gram.T.astype(done.dtype)

        @pl.when(gives(l, lax.div(j, mine)))
        def _():
            turned[kk, j] = gram.T.astype(turned.dtype)

            @pl.when(sends)
            def _():
                mirror(kk, j).start()

    def finish(n, sends):
        def one(p, q):
            @pl.when(closed(p, q))
            def _():
                close(p, q, sends)

        loop(n + 1, lambda q: one(n, q))
        loop(n, lambda p: one(p, n))

    soon = units - BEHIND
    prompt = jnp.logical_or(on_diagonal, jnp.logical_and(mirrors, jnp.abs(c - r) < 2))

    def send_mirrored(p):
        i = order(p)

        def one(q):
            j = order(q)

            @pl.when(jnp.logical_and(closed(p, q), gives(l, lax.div(j, mine))))
            def _():
                mirror(lax.rem(i, mine), j).start()

        loop(soon, one)

    def gather_rows(n):
        u = order(n)
        k = lax.div(u, split)
        for h in range(SUB):

            @pl.when(jnp.logical_and(n >= split, n < limit))
            def _():
                along(0, u, n, h).wait_recv()
                for side in range(2):
                    onward = k < c if side == 0 else k > c

                    @pl.when(jnp.logical_and(onward, goes_on(side, u)))
                    def _():
                        along(side, u, n, h).start()

            @pl.when(node == 0)
            def _():
                for bit in reversed(range(bits)):
                    down(bit, n, h).start()

    def gather_columns(n):
        @pl.when(node != 0)
        def _():
            for h in range(SUB):
                down(0, n, h).wait_recv()
                for bit in reversed(range(bits)):

                    @pl.when(has_child(bit))
                    def _():
                        down(bit, n, h).start()

    def row_norms(n):
        a = rb[n].astype(jnp.float32)
        rn[n] = jnp.broadcast_to(jnp.sum(a * a, axis=1, keepdims=True), rn.shape[1:])

    def column_norms(n):
        b = rb[base + n].astype(jnp.float32)
        s = jnp.broadcast_to(jnp.sum(b * b, axis=1, keepdims=True), (m, 128))
        cn[n] = s.T[:8]

    def step(n):
        gather_rows(n)

        @pl.when(n < limit)
        def _():
            row_norms(n)
            loop(lax.div(n, 2), lambda t: wide(n, t))

            @pl.when(lax.rem(n, 2) == 1)
            def _():
                keep(n, n - 1, inner_of(rb[n], rb[base + n - 1]), holds(n))

        @pl.when(holds(n - 1))
        def _():
            release(n - 1)

        gather_columns(n)
        column_norms(n)
        count = jnp.minimum(n + 1, limit)
        loop(lax.div(count, 2), lambda t: tall(t, n))

        @pl.when(lax.rem(count, 2) == 1)
        def _():
            keep(count - 1, n, inner_of(rb[count - 1], rb[base + n]))

        @pl.when(n >= BEHIND)
        def _():
            finish(n - BEHIND, prompt)

    loop(units, step)

    @pl.when(jnp.logical_not(prompt))
    def _():
        loop(soon, send_mirrored)

    loop(BEHIND, lambda o: finish(units - BEHIND + o, True))

    def landed(t, carry):
        kk, i = lax.div(t, units), lax.rem(t, units)

        @pl.when(takes(l, lax.div(i, mine)))
        def _():
            pltpu.make_async_remote_copy(
                turned.at[0, 0], done.at[kk, i], m_send.at[0, 0], m_recv.at[kk, i],
                device_id={"row": c, "col": r, "lag": lax.div(i, mine)},
                device_id_type=MESH,
            ).wait_recv()

        return carry

    lax.fori_loop(0, mine * units, landed, 0)

    def lay(kk, carry):
        for j in range(units):
            out_ref[pl.ds(kk * m, m), j * m : (j + 1) * m] = done[kk, j]
        return carry

    lax.fori_loop(0, mine, lay, 0)
    put = pltpu.make_async_copy(out_ref, result, out_sem)
    put.start()

    def drain(p, carry):
        u = order(p)
        k = lax.div(u, split)
        got_it = jnp.logical_or(k == c, p < limit)
        for h in range(SUB):

            @pl.when(jnp.logical_and(got_it, jnp.logical_and(k <= c, goes_on(0, u))))
            def _():
                along(0, u, p, h).wait_send()

            @pl.when(jnp.logical_and(got_it, jnp.logical_and(k >= c, goes_on(1, u))))
            def _():
                along(1, u, p, h).wait_send()

            for bit in range(bits):

                @pl.when(has_child(bit))
                def _():
                    down(bit, p, h).wait_send()

        def each(q, carry):
            @pl.when(sent(p, q))
            def _():
                across(u, order(q)).wait_send()

            return carry

        lax.fori_loop(0, units, each, 0)

        return carry

    lax.fori_loop(0, units, drain, 0)

    def gone(t, carry):
        kk, j = lax.div(t, units), lax.rem(t, units)

        @pl.when(gives(l, lax.div(j, mine)))
        def _():
            mirror(kk, j).wait_send()

        return carry

    lax.fori_loop(0, mine * units, gone, 0)
    put.wait()


def on_device(rows, cols, lags, trajectories, pair_live):
    held, width = trajectories.shape
    split = SPLIT if held % (SPLIT * 128) == 0 else 1
    m = held // split
    units = cols * split
    mine = units // lags
    bits = rows.bit_length() - 1
    dma = pltpu.SemaphoreType.DMA
    return pl.pallas_call(
        functools.partial(kernel, rows, cols, lags, split, width * lags),
        out_shape=jax.ShapeDtypeStruct((mine * m, units * m), jnp.bfloat16),
        in_specs=[
            pl.BlockSpec(memory_space=pl.ANY),
            pl.BlockSpec(memory_space=pltpu.SMEM),
        ],
        out_specs=pl.BlockSpec(memory_space=pl.ANY),
        scratch_shapes=[
            pltpu.VMEM((mine * m, units * m), jnp.bfloat16),
            dma,
            pltpu.VMEM((2 * units, m, width), jnp.bfloat16),
            pltpu.VMEM((units, m, 128), jnp.float32),
            pltpu.VMEM((units, 8, m), jnp.float32),
            pltpu.VMEM((units, units, m, m), jnp.float32),
            pltpu.VMEM((lags - 1, mine, units, m, m), jnp.float32),
            pltpu.VMEM((mine, units, m, m), jnp.bfloat16),
            pltpu.VMEM((mine, units, m, m), jnp.bfloat16),
            dma,
            dma((2, units, SUB)),
            dma((units, SUB)),
            dma((bits, units, SUB)),
            dma((units, SUB)),
            dma((units, units)),
            dma((lags - 1, mine, units)),
            dma((mine, units)),
            dma((mine, units)),
        ],
        compiler_params=pltpu.CompilerParams(
            collective_id=0, has_side_effects=True, vmem_limit_bytes=60 * 2**20
        ),
    )(trajectories.reshape(split, m, width), pair_live)


def solution(mesh):
    size = mesh.shape
    return jax.shard_map(
        functools.partial(on_device, size["row"], size["col"], size["lag"]),
        mesh=mesh,
        in_specs=(P(("row", "col"), "lag"), P()),
        out_specs=P(("row", "lag"), "col"),
        check_vma=False,
    )
```

```python
import functools

import jax
import jax.numpy as jnp
from jax import lax
from jax.experimental import pallas as pl
from jax.experimental.pallas import tpu as pltpu
from jax.sharding import PartitionSpec as P

MESH = pl.DeviceIdType.MESH
SPLIT = 2
SUB = 2
BEHIND = 1
NT_DIMS = (((1,), (1,)), ((), ()))


def kernel(
    rows, cols, lags, split, samples,
    x_ref, live_ref, result,
    out_ref, out_sem, rb, rn, cn, tile, got, turned, done,
    own_sem, z_send, z_recv, c_send, c_recv, t_send, t_recv, m_send, m_recv,
):
    r, c, l = lax.axis_index("row"), lax.axis_index("col"), lax.axis_index("lag")
    units = cols * split
    m = rb.shape[1]
    mine = units // lags
    bits = rows.bit_length() - 1
    node = lax.bitwise_xor(r, c)
    base = jnp.where(node == 0, 0, units)
    chunk = m // SUB

    at_end = jnp.logical_or(c == 0, c == cols - 1)
    inside = jnp.logical_and(r > 0, r < rows - 1)
    partial = jnp.logical_and(inside, at_end)
    limit = jnp.where(partial, mine, units)
    mirrors = jnp.logical_not(jnp.logical_or(inside, at_end))
    on_diagonal = r == c
    turns = jnp.logical_and(on_diagonal, jnp.logical_not(at_end))
    swaps = jnp.logical_and(inside, jnp.logical_not(jnp.logical_or(at_end, on_diagonal)))
    paired = jnp.logical_not(jnp.logical_or(on_diagonal, jnp.logical_and(at_end, jnp.logical_not(partial))))

    first = jnp.where(on_diagonal, 2 * c < cols, c < r)
    early = jnp.where(first, 0, lags - 1)
    late = lags - 1 - early

    def near_lag(end):
        return jnp.where(end == 0, 0, lags - 1)

    def gives(a, b):
        given = jnp.logical_and(mirrors, b != near_lag(r))
        if lags == 1:
            return given
        swap = jnp.logical_and(swaps, jnp.logical_and(a == early, b == early))
        turn = jnp.logical_and(turns, jnp.logical_and(a == early, b != early))
        return jnp.logical_or(given, jnp.logical_or(swap, turn))

    def takes(a, b):
        taken = jnp.logical_and(partial, a != near_lag(c))
        if lags == 1:
            return taken
        swap = jnp.logical_and(swaps, jnp.logical_and(a == late, b == late))
        turn = jnp.logical_and(turns, jnp.logical_and(a != early, b == early))
        return jnp.logical_or(taken, jnp.logical_or(swap, turn))

    def double(p, q, a, b):
        return jnp.logical_and(on_diagonal, jnp.logical_and(a == b, p < q))

    def sent(p, q):
        a, b = lax.div(order(p), mine), lax.div(order(q), mine)
        skipped = jnp.logical_or(takes(a, b), double(p, q, a, b))
        return jnp.logical_and(a != l, jnp.logical_not(skipped))

    def closed(p, q):
        a, b = lax.div(order(p), mine), lax.div(order(q), mine)
        skipped = jnp.logical_or(takes(a, b), double(p, q, a, b))
        return jnp.logical_and(a == l, jnp.logical_not(skipped))

    def place(u, where):
        k = lax.div(u, split)
        e = u - k * split
        left, right = where, cols - 1 - where
        d = jnp.abs(k - where)
        both = jnp.logical_and(d <= left, d <= right)
        before = split * (1 + jnp.minimum(d - 1, left) + jnp.minimum(d - 1, right))
        second = (k > where) != (left < right)
        far = before + jnp.where(both, 2 * e + jnp.where(second, 1, 0), e)
        return jnp.where(d == 0, e, far)

    def unit_of(p):
        left, right = c, cols - 1 - c
        near = jnp.minimum(left, right)
        p1 = jnp.maximum(p - split, 0)
        p2 = jnp.maximum(p1 - 2 * split * near, 0)
        close = p1 < 2 * split * near
        d1 = p1 // (2 * split)
        rest = p1 - d1 * (2 * split)
        e1 = rest // 2
        s1 = jnp.where(left < right, 1 - rest + 2 * e1, rest - 2 * e1)
        d2 = p2 // split
        e2 = p2 - d2 * split
        s2 = jnp.where(left < right, 1, 0)
        d = jnp.where(close, d1 + 1, d2 + near + 1)
        e = jnp.where(close, e1, e2)
        s = jnp.where(close, s1, s2)
        k = jnp.where(s == 0, c - d, c + d)
        k = jnp.clip(k, 0, cols - 1)
        return jnp.where(p < split, c * split + p, k * split + e)

    def along(side, u, p, h, src=None):
        to = jnp.clip(c + 1 - 2 * side, 0, cols - 1)
        rows_of = pl.ds(h * chunk, chunk)
        return pltpu.make_async_remote_copy(
            rb.at[p, rows_of] if src is None else src.at[p, rows_of],
            rb.at[place(u, to), rows_of],
            z_send.at[side, u, h], z_recv.at[u, h],
            device_id={"col": to}, device_id_type=MESH,
        )

    def down(bit, p, h):
        rows_of = pl.ds(h * chunk, chunk)
        return pltpu.make_async_remote_copy(
            rb.at[base + p, rows_of], rb.at[units + p, rows_of],
            c_send.at[bit, p, h], c_recv.at[p, h],
            device_id={"row": lax.bitwise_xor(r, 1 << bit)}, device_id_type=MESH,
        )

    def has_child(bit):
        return lax.rem(node, 2 << bit) == 0

    def across(i, j):
        owner = lax.div(i, mine)
        hop = lax.rem(owner - l + lags, lags)
        slot = jnp.maximum(hop - 1, 0)
        return pltpu.make_async_remote_copy(
            tile.at[i, j], got.at[slot, lax.rem(i, mine), j],
            t_send.at[i, j], t_recv.at[slot, lax.rem(i, mine), j],
            device_id={"lag": owner}, device_id_type=MESH,
        )

    def mirror(kk, j):
        i = l * mine + kk
        return pltpu.make_async_remote_copy(
            turned.at[kk, j], done.at[lax.rem(j, mine), i],
            m_send.at[kk, j], m_recv.at[lax.rem(j, mine), i],
            device_id={"row": c, "col": r, "lag": lax.div(j, mine)}, device_id_type=MESH,
        )

    at = [unit_of(jnp.int32(p)) for p in range(units)]

    def order(p):
        u = at[-1]
        for i in range(units - 1):
            u = jnp.where(p == i, at[i], u)
        return u

    own = pltpu.make_async_copy(x_ref, rb.at[pl.ds(0, split)], own_sem)
    own.start()

    barrier = pltpu.get_barrier_semaphore()
    for j in range(1, rows):
        pl.semaphore_signal(
            barrier, device_id={"row": lax.rem(r + j, rows)}, device_id_type=MESH
        )
    for j in range(1, lags):
        pl.semaphore_signal(
            barrier, device_id={"lag": lax.rem(l + j, lags)}, device_id_type=MESH
        )

    @pl.when(c > 0)
    def _():
        pl.semaphore_signal(barrier, device_id={"col": c - 1}, device_id_type=MESH)

    @pl.when(c < cols - 1)
    def _():
        pl.semaphore_signal(barrier, device_id={"col": c + 1}, device_id_type=MESH)

    @pl.when(paired)
    def _():
        for o in range(lags):
            pl.semaphore_signal(
                barrier, device_id={"row": c, "col": r, "lag": o}, device_id_type=MESH
            )

    beside = jnp.where(at_end, 1, 2) + jnp.where(paired, lags, 0)
    pl.semaphore_wait(barrier, rows - 1 + lags - 1 + beside)

    def goes_on(side, u):
        a = lax.div(u, mine)
        if side == 0:
            return c < jnp.where(jnp.logical_and(inside, a != lags - 1), cols - 2, cols - 1)
        return c > jnp.where(jnp.logical_and(inside, a != 0), 1, 0)

    for side in range(2):
        for e in range(split):

            @pl.when(goes_on(side, c * split + e))
            def _():
                for h in range(SUB):
                    along(side, c * split + e, e, h, x_ref).start()

    own.wait()
    live = live_ref[r, c].astype(jnp.float32)

    def inner_of(a, b):
        return lax.dot_general(a, b, NT_DIMS, preferred_element_type=jnp.float32)

    def two(at):
        return rb[pl.ds(at, 2)].reshape(2 * m, rb.shape[2])

    def keep(p, q, inner):
        i, j = order(p), order(q)
        tile[i, j] = rn[p][:, :1] + cn[q][:1] - 2.0 * inner

        @pl.when(sent(p, q))
        def _():
            across(i, j).start()

    def wide(n, t):
        inner = inner_of(rb[n], two(base + 2 * t))
        for j in range(2):
            keep(n, 2 * t + j, inner[:, j * m : (j + 1) * m])

    def tall(s, n):
        inner = inner_of(two(2 * s), rb[base + n])
        for i in range(2):
            keep(2 * s + i, n, inner[i * m : (i + 1) * m])

    def loop(count, body):
        def one(t, carry):
            body(t)
            return carry

        lax.fori_loop(0, count, one, 0)

    def close(p, q, sends):
        i, j = order(p), order(q)
        kk = lax.rem(i, mine)
        total = tile[i, j]
        for o in range(lags - 1):
            pltpu.make_async_remote_copy(
                tile.at[i, j], got.at[o, kk, j], t_send.at[i, j], t_recv.at[o, kk, j],
                device_id={"lag": lax.rem(l + 1, lags)}, device_id_type=MESH,
            ).wait_recv()
            total = total + got[o, kk, j]
        gram = jnp.exp(-2.0 * total / samples) * live
        done[kk, j] = gram.astype(done.dtype)

        @pl.when(double(q, p, lax.div(i, mine), lax.div(j, mine)))
        def _():
            done[lax.rem(j, mine), i] = gram.T.astype(done.dtype)

        @pl.when(gives(l, lax.div(j, mine)))
        def _():
            turned[kk, j] = gram.T.astype(turned.dtype)

            @pl.when(sends)
            def _():
                mirror(kk, j).start()

    def finish(n, sends):
        def one(p, q):
            @pl.when(closed(p, q))
            def _():
                close(p, q, sends)

        loop(n + 1, lambda q: one(n, q))
        loop(n, lambda p: one(p, n))

    soon = units - BEHIND
    prompt = jnp.logical_or(on_diagonal, jnp.logical_and(mirrors, jnp.abs(c - r) < 2))

    def send_mirrored(p):
        i = order(p)

        def one(q):
            j = order(q)

            @pl.when(jnp.logical_and(closed(p, q), gives(l, lax.div(j, mine))))
            def _():
                mirror(lax.rem(i, mine), j).start()

        loop(soon, one)

    def gather_rows(n):
        u = order(n)
        k = lax.div(u, split)
        for h in range(SUB):

            @pl.when(jnp.logical_and(n >= split, n < limit))
            def _():
                along(0, u, n, h).wait_recv()
                for side in range(2):
                    onward = k < c if side == 0 else k > c

                    @pl.when(jnp.logical_and(onward, goes_on(side, u)))
                    def _():
                        along(side, u, n, h).start()

            @pl.when(node == 0)
            def _():
                for bit in reversed(range(bits)):
                    down(bit, n, h).start()

    def gather_columns(n):
        @pl.when(node != 0)
        def _():
            for h in range(SUB):
                down(0, n, h).wait_recv()
                for bit in reversed(range(bits)):

                    @pl.when(has_child(bit))
                    def _():
                        down(bit, n, h).start()

    def row_norms(n):
        a = rb[n].astype(jnp.float32)
        rn[n] = jnp.broadcast_to(jnp.sum(a * a, axis=1, keepdims=True), rn.shape[1:])

    def column_norms(n):
        @pl.when(node == 0)
        def _():
            cn[n] = rn[n].T[:8]

        @pl.when(node != 0)
        def _():
            b = rb[units + n].astype(jnp.float32)
            s = jnp.broadcast_to(jnp.sum(b * b, axis=1, keepdims=True), (m, 128))
            cn[n] = s.T[:8]

    def step(n):
        gather_rows(n)

        @pl.when(n < limit)
        def _():
            row_norms(n)
            loop(lax.div(n, 2), lambda t: wide(n, t))

            @pl.when(lax.rem(n, 2) == 1)
            def _():
                keep(n, n - 1, inner_of(rb[n], rb[base + n - 1]))

        gather_columns(n)
        column_norms(n)
        count = jnp.minimum(n + 1, limit)
        loop(lax.div(count, 2), lambda t: tall(t, n))

        @pl.when(lax.rem(count, 2) == 1)
        def _():
            keep(count - 1, n, inner_of(rb[count - 1], rb[base + n]))

        @pl.when(n >= BEHIND)
        def _():
            finish(n - BEHIND, prompt)

    loop(units, step)

    @pl.when(jnp.logical_not(prompt))
    def _():
        loop(soon, send_mirrored)

    loop(BEHIND, lambda o: finish(units - BEHIND + o, True))

    def landed(t, carry):
        kk, i = lax.div(t, units), lax.rem(t, units)

        @pl.when(takes(l, lax.div(i, mine)))
        def _():
            pltpu.make_async_remote_copy(
                turned.at[0, 0], done.at[kk, i], m_send.at[0, 0], m_recv.at[kk, i],
                device_id={"row": c, "col": r, "lag": lax.div(i, mine)},
                device_id_type=MESH,
            ).wait_recv()

        return carry

    lax.fori_loop(0, mine * units, landed, 0)

    def lay(kk, carry):
        for j in range(units):
            out_ref[pl.ds(kk * m, m), j * m : (j + 1) * m] = done[kk, j]
        return carry

    lax.fori_loop(0, mine, lay, 0)
    put = pltpu.make_async_copy(out_ref, result, out_sem)
    put.start()

    def drain(p, carry):
        u = order(p)
        k = lax.div(u, split)
        got_it = jnp.logical_or(k == c, p < limit)
        for h in range(SUB):

            @pl.when(jnp.logical_and(got_it, jnp.logical_and(k <= c, goes_on(0, u))))
            def _():
                along(0, u, p, h).wait_send()

            @pl.when(jnp.logical_and(got_it, jnp.logical_and(k >= c, goes_on(1, u))))
            def _():
                along(1, u, p, h).wait_send()

            for bit in range(bits):

                @pl.when(has_child(bit))
                def _():
                    down(bit, p, h).wait_send()

        def each(q, carry):
            @pl.when(sent(p, q))
            def _():
                across(u, order(q)).wait_send()

            return carry

        lax.fori_loop(0, units, each, 0)

        return carry

    lax.fori_loop(0, units, drain, 0)

    def gone(t, carry):
        kk, j = lax.div(t, units), lax.rem(t, units)

        @pl.when(gives(l, lax.div(j, mine)))
        def _():
            mirror(kk, j).wait_send()

        return carry

    lax.fori_loop(0, mine * units, gone, 0)
    put.wait()


def on_device(rows, cols, lags, trajectories, pair_live):
    held, width = trajectories.shape
    split = SPLIT if held % (SPLIT * 128) == 0 else 1
    m = held // split
    units = cols * split
    mine = units // lags
    bits = rows.bit_length() - 1
    dma = pltpu.SemaphoreType.DMA
    return pl.pallas_call(
        functools.partial(kernel, rows, cols, lags, split, width * lags),
        out_shape=jax.ShapeDtypeStruct((mine * m, units * m), jnp.bfloat16),
        in_specs=[
            pl.BlockSpec(memory_space=pl.ANY),
            pl.BlockSpec(memory_space=pltpu.SMEM),
        ],
        out_specs=pl.BlockSpec(memory_space=pl.ANY),
        scratch_shapes=[
            pltpu.VMEM((mine * m, units * m), jnp.bfloat16),
            dma,
            pltpu.VMEM((2 * units, m, width), jnp.bfloat16),
            pltpu.VMEM((units, m, 128), jnp.float32),
            pltpu.VMEM((units, 8, m), jnp.float32),
            pltpu.VMEM((units, units, m, m), jnp.float32),
            pltpu.VMEM((lags - 1, mine, units, m, m), jnp.float32),
            pltpu.VMEM((mine, units, m, m), jnp.bfloat16),
            pltpu.VMEM((mine, units, m, m), jnp.bfloat16),
            dma,
            dma((2, units, SUB)),
            dma((units, SUB)),
            dma((bits, units, SUB)),
            dma((units, SUB)),
            dma((units, units)),
            dma((lags - 1, mine, units)),
            dma((mine, units)),
            dma((mine, units)),
        ],
        compiler_params=pltpu.CompilerParams(
            collective_id=0, has_side_effects=True, vmem_limit_bytes=60 * 2**20
        ),
    )(trajectories.reshape(split, m, width), pair_live)


def solution(mesh):
    size = mesh.shape
    return jax.shard_map(
        functools.partial(on_device, size["row"], size["col"], size["lag"]),
        mesh=mesh,
        in_specs=(P(("row", "col"), "lag"), P()),
        out_specs=P(("row", "lag"), "col"),
        check_vma=False,
    )
```

```python
import functools

import jax
import jax.numpy as jnp
from jax import lax
from jax.experimental import pallas as pl
from jax.experimental.pallas import tpu as pltpu
from jax.sharding import PartitionSpec as P

MESH = pl.DeviceIdType.MESH
SPLIT = 2
SUB = 2
BEHIND = 1
NT_DIMS = (((1,), (1,)), ((), ()))


def kernel(
    rows, cols, lags, split, samples,
    x_ref, live_ref, result,
    out_ref, out_sem, rb, rn, cn, tile, got, turned, done,
    own_sem, z_send, z_recv, c_send, c_recv, t_send, t_recv, m_send, m_recv,
):
    r, c, l = lax.axis_index("row"), lax.axis_index("col"), lax.axis_index("lag")
    units = cols * split
    m = rb.shape[1]
    mine = units // lags
    bits = rows.bit_length() - 1
    node = lax.bitwise_xor(r, c)
    base = jnp.where(node == 0, 0, units)
    chunk = m // SUB

    at_end = jnp.logical_or(c == 0, c == cols - 1)
    inside = jnp.logical_and(r > 0, r < rows - 1)
    partial = jnp.logical_and(inside, at_end)
    limit = jnp.where(partial, mine, units)
    mirrors = jnp.logical_not(jnp.logical_or(inside, at_end))
    on_diagonal = r == c
    turns = jnp.logical_and(on_diagonal, jnp.logical_not(at_end))
    swaps = jnp.logical_and(inside, jnp.logical_not(jnp.logical_or(at_end, on_diagonal)))
    paired = jnp.logical_not(jnp.logical_or(on_diagonal, jnp.logical_and(at_end, jnp.logical_not(partial))))

    first = jnp.where(on_diagonal, 2 * c < cols, c < r)
    early = jnp.where(first, 0, lags - 1)
    late = lags - 1 - early

    def near_lag(end):
        return jnp.where(end == 0, 0, lags - 1)

    def gives(a, b):
        given = jnp.logical_and(mirrors, b != near_lag(r))
        if lags == 1:
            return given
        swap = jnp.logical_and(swaps, jnp.logical_and(a == early, b == early))
        turn = jnp.logical_and(turns, jnp.logical_and(a == early, b != early))
        return jnp.logical_or(given, jnp.logical_or(swap, turn))

    def takes(a, b):
        taken = jnp.logical_and(partial, a != near_lag(c))
        if lags == 1:
            return taken
        swap = jnp.logical_and(swaps, jnp.logical_and(a == late, b == late))
        turn = jnp.logical_and(turns, jnp.logical_and(a != early, b == early))
        return jnp.logical_or(taken, jnp.logical_or(swap, turn))

    def double(p, q, a, b):
        return jnp.logical_and(on_diagonal, jnp.logical_and(a == b, p < q))

    def sent(p, q):
        a, b = lax.div(order(p), mine), lax.div(order(q), mine)
        skipped = jnp.logical_or(takes(a, b), double(p, q, a, b))
        return jnp.logical_and(a != l, jnp.logical_not(skipped))

    def closed(p, q):
        a, b = lax.div(order(p), mine), lax.div(order(q), mine)
        skipped = jnp.logical_or(takes(a, b), double(p, q, a, b))
        return jnp.logical_and(a == l, jnp.logical_not(skipped))

    def place(u, where):
        k = lax.div(u, split)
        e = u - k * split
        left, right = where, cols - 1 - where
        d = jnp.abs(k - where)
        both = jnp.logical_and(d <= left, d <= right)
        before = split * (1 + jnp.minimum(d - 1, left) + jnp.minimum(d - 1, right))
        second = (k > where) != (left < right)
        far = before + jnp.where(both, 2 * e + jnp.where(second, 1, 0), e)
        return jnp.where(d == 0, e, far)

    def unit_of(p):
        left, right = c, cols - 1 - c
        near = jnp.minimum(left, right)
        p1 = jnp.maximum(p - split, 0)
        p2 = jnp.maximum(p1 - 2 * split * near, 0)
        close = p1 < 2 * split * near
        d1 = p1 // (2 * split)
        rest = p1 - d1 * (2 * split)
        e1 = rest // 2
        s1 = jnp.where(left < right, 1 - rest + 2 * e1, rest - 2 * e1)
        d2 = p2 // split
        e2 = p2 - d2 * split
        s2 = jnp.where(left < right, 1, 0)
        d = jnp.where(close, d1 + 1, d2 + near + 1)
        e = jnp.where(close, e1, e2)
        s = jnp.where(close, s1, s2)
        k = jnp.where(s == 0, c - d, c + d)
        k = jnp.clip(k, 0, cols - 1)
        return jnp.where(p < split, c * split + p, k * split + e)

    def along(side, u, p, h, src=None):
        to = jnp.clip(c + 1 - 2 * side, 0, cols - 1)
        rows_of = pl.ds(h * chunk, chunk)
        return pltpu.make_async_remote_copy(
            rb.at[p, rows_of] if src is None else src.at[p, rows_of],
            rb.at[place(u, to), rows_of],
            z_send.at[side, u, h], z_recv.at[u, h],
            device_id={"col": to}, device_id_type=MESH,
        )

    def down(bit, p, h):
        rows_of = pl.ds(h * chunk, chunk)
        return pltpu.make_async_remote_copy(
            rb.at[base + p, rows_of], rb.at[units + p, rows_of],
            c_send.at[bit, p, h], c_recv.at[p, h],
            device_id={"row": lax.bitwise_xor(r, 1 << bit)}, device_id_type=MESH,
        )

    def has_child(bit):
        return lax.rem(node, 2 << bit) == 0

    def across(i, j):
        owner = lax.div(i, mine)
        hop = lax.rem(owner - l + lags, lags)
        slot = jnp.maximum(hop - 1, 0)
        return pltpu.make_async_remote_copy(
            tile.at[i, j], got.at[slot, lax.rem(i, mine), j],
            t_send.at[i, j], t_recv.at[slot, lax.rem(i, mine), j],
            device_id={"lag": owner}, device_id_type=MESH,
        )

    def mirror(kk, j):
        i = l * mine + kk
        return pltpu.make_async_remote_copy(
            turned.at[kk, j], done.at[lax.rem(j, mine), i],
            m_send.at[kk, j], m_recv.at[lax.rem(j, mine), i],
            device_id={"row": c, "col": r, "lag": lax.div(j, mine)}, device_id_type=MESH,
        )

    at = [unit_of(jnp.int32(p)) for p in range(units)]

    def order(p):
        u = at[-1]
        for i in range(units - 1):
            u = jnp.where(p == i, at[i], u)
        return u

    own = pltpu.make_async_copy(x_ref, rb.at[pl.ds(0, split)], own_sem)
    own.start()

    barrier = pltpu.get_barrier_semaphore()
    for j in range(1, rows):
        pl.semaphore_signal(
            barrier, device_id={"row": lax.rem(r + j, rows)}, device_id_type=MESH
        )
    for j in range(1, lags):
        pl.semaphore_signal(
            barrier, device_id={"lag": lax.rem(l + j, lags)}, device_id_type=MESH
        )

    @pl.when(c > 0)
    def _():
        pl.semaphore_signal(barrier, device_id={"col": c - 1}, device_id_type=MESH)

    @pl.when(c < cols - 1)
    def _():
        pl.semaphore_signal(barrier, device_id={"col": c + 1}, device_id_type=MESH)

    @pl.when(paired)
    def _():
        for o in range(lags):
            pl.semaphore_signal(
                barrier, device_id={"row": c, "col": r, "lag": o}, device_id_type=MESH
            )

    beside = jnp.where(at_end, 1, 2) + jnp.where(paired, lags, 0)
    pl.semaphore_wait(barrier, rows - 1 + lags - 1 + beside)

    def goes_on(side, u):
        a = lax.div(u, mine)
        if side == 0:
            return c < jnp.where(jnp.logical_and(inside, a != lags - 1), cols - 2, cols - 1)
        return c > jnp.where(jnp.logical_and(inside, a != 0), 1, 0)

    for e in range(split):
        for side in range(2):

            @pl.when(goes_on(side, c * split + e))
            def _():
                for h in range(SUB):
                    along(side, c * split + e, e, h, x_ref).start()

    own.wait()
    live = live_ref[r, c].astype(jnp.float32)

    def inner_of(a, b):
        return lax.dot_general(a, b, NT_DIMS, preferred_element_type=jnp.float32)

    def two(at):
        return rb[pl.ds(at, 2)].reshape(2 * m, rb.shape[2])

    def keep(p, q, inner):
        i, j = order(p), order(q)
        tile[i, j] = rn[p][:, :1] + cn[q][:1] - 2.0 * inner

        @pl.when(sent(p, q))
        def _():
            across(i, j).start()

    def wide(n, t):
        inner = inner_of(rb[n], two(base + 2 * t))
        for j in range(2):
            keep(n, 2 * t + j, inner[:, j * m : (j + 1) * m])

    def tall(s, n):
        inner = inner_of(two(2 * s), rb[base + n])
        for i in range(2):
            keep(2 * s + i, n, inner[i * m : (i + 1) * m])

    def loop(count, body):
        def one(t, carry):
            body(t)
            return carry

        lax.fori_loop(0, count, one, 0)

    def close(p, q, sends):
        i, j = order(p), order(q)
        kk = lax.rem(i, mine)
        total = tile[i, j]
        for o in range(lags - 1):
            pltpu.make_async_remote_copy(
                tile.at[i, j], got.at[o, kk, j], t_send.at[i, j], t_recv.at[o, kk, j],
                device_id={"lag": lax.rem(l + 1, lags)}, device_id_type=MESH,
            ).wait_recv()
            total = total + got[o, kk, j]
        gram = jnp.exp(-2.0 * total / samples) * live
        done[kk, j] = gram.astype(done.dtype)

        @pl.when(double(q, p, lax.div(i, mine), lax.div(j, mine)))
        def _():
            done[lax.rem(j, mine), i] = gram.T.astype(done.dtype)

        @pl.when(gives(l, lax.div(j, mine)))
        def _():
            turned[kk, j] = gram.T.astype(turned.dtype)

            @pl.when(sends)
            def _():
                mirror(kk, j).start()

    def finish(n, sends):
        def one(p, q):
            @pl.when(closed(p, q))
            def _():
                close(p, q, sends)

        loop(n + 1, lambda q: one(n, q))
        loop(n, lambda p: one(p, n))

    soon = units - BEHIND
    prompt = jnp.logical_or(on_diagonal, jnp.logical_and(mirrors, jnp.abs(c - r) < 2))

    def send_mirrored(p):
        i = order(p)

        def one(q):
            j = order(q)

            @pl.when(jnp.logical_and(closed(p, q), gives(l, lax.div(j, mine))))
            def _():
                mirror(lax.rem(i, mine), j).start()

        loop(soon, one)

    def gather_rows(n):
        u = order(n)
        k = lax.div(u, split)
        for h in range(SUB):

            @pl.when(jnp.logical_and(n >= split, n < limit))
            def _():
                along(0, u, n, h).wait_recv()
                for side in range(2):
                    onward = k < c if side == 0 else k > c

                    @pl.when(jnp.logical_and(onward, goes_on(side, u)))
                    def _():
                        along(side, u, n, h).start()

            @pl.when(node == 0)
            def _():
                for bit in reversed(range(bits)):
                    down(bit, n, h).start()

    def gather_columns(n):
        @pl.when(node != 0)
        def _():
            for h in range(SUB):
                down(0, n, h).wait_recv()
                for bit in reversed(range(bits)):

                    @pl.when(has_child(bit))
                    def _():
                        down(bit, n, h).start()

    def row_norms(n):
        a = rb[n].astype(jnp.float32)
        rn[n] = jnp.broadcast_to(jnp.sum(a * a, axis=1, keepdims=True), rn.shape[1:])

    def column_norms(n):
        @pl.when(node == 0)
        def _():
            cn[n] = rn[n].T[:8]

        @pl.when(node != 0)
        def _():
            b = rb[units + n].astype(jnp.float32)
            s = jnp.broadcast_to(jnp.sum(b * b, axis=1, keepdims=True), (m, 128))
            cn[n] = s.T[:8]

    def step(n):
        gather_rows(n)

        @pl.when(n < limit)
        def _():
            row_norms(n)
            loop(lax.div(n, 2), lambda t: wide(n, t))

            @pl.when(lax.rem(n, 2) == 1)
            def _():
                keep(n, n - 1, inner_of(rb[n], rb[base + n - 1]))

        gather_columns(n)
        column_norms(n)
        count = jnp.minimum(n + 1, limit)
        loop(lax.div(count, 2), lambda t: tall(t, n))

        @pl.when(lax.rem(count, 2) == 1)
        def _():
            keep(count - 1, n, inner_of(rb[count - 1], rb[base + n]))

        @pl.when(n >= BEHIND)
        def _():
            finish(n - BEHIND, prompt)

    loop(units, step)

    @pl.when(jnp.logical_not(prompt))
    def _():
        loop(soon, send_mirrored)

    loop(BEHIND, lambda o: finish(units - BEHIND + o, True))

    def landed(t, carry):
        kk, i = lax.div(t, units), lax.rem(t, units)

        @pl.when(takes(l, lax.div(i, mine)))
        def _():
            pltpu.make_async_remote_copy(
                turned.at[0, 0], done.at[kk, i], m_send.at[0, 0], m_recv.at[kk, i],
                device_id={"row": c, "col": r, "lag": lax.div(i, mine)},
                device_id_type=MESH,
            ).wait_recv()

        return carry

    lax.fori_loop(0, mine * units, landed, 0)

    def put(kk):
        rows_of = pl.ds(kk * m, m)
        return pltpu.make_async_copy(
            out_ref.at[rows_of], result.at[rows_of], out_sem.at[kk]
        )

    def lay(kk, carry):
        for j in range(units):
            out_ref[pl.ds(kk * m, m), j * m : (j + 1) * m] = done[kk, j]
        put(kk).start()
        return carry

    lax.fori_loop(0, mine, lay, 0)

    def drain(p, carry):
        u = order(p)
        k = lax.div(u, split)
        got_it = jnp.logical_or(k == c, p < limit)
        for h in range(SUB):

            @pl.when(jnp.logical_and(got_it, jnp.logical_and(k <= c, goes_on(0, u))))
            def _():
                along(0, u, p, h).wait_send()

            @pl.when(jnp.logical_and(got_it, jnp.logical_and(k >= c, goes_on(1, u))))
            def _():
                along(1, u, p, h).wait_send()

            for bit in range(bits):

                @pl.when(has_child(bit))
                def _():
                    down(bit, p, h).wait_send()

        def each(q, carry):
            @pl.when(sent(p, q))
            def _():
                across(u, order(q)).wait_send()

            return carry

        lax.fori_loop(0, units, each, 0)

        return carry

    lax.fori_loop(0, units, drain, 0)

    def gone(t, carry):
        kk, j = lax.div(t, units), lax.rem(t, units)

        @pl.when(gives(l, lax.div(j, mine)))
        def _():
            mirror(kk, j).wait_send()

        return carry

    lax.fori_loop(0, mine * units, gone, 0)
    loop(mine, lambda kk: put(kk).wait())


def on_device(rows, cols, lags, trajectories, pair_live):
    held, width = trajectories.shape
    split = SPLIT if held % (SPLIT * 128) == 0 else 1
    m = held // split
    units = cols * split
    mine = units // lags
    bits = rows.bit_length() - 1
    dma = pltpu.SemaphoreType.DMA
    return pl.pallas_call(
        functools.partial(kernel, rows, cols, lags, split, width * lags),
        out_shape=jax.ShapeDtypeStruct((mine * m, units * m), jnp.bfloat16),
        in_specs=[
            pl.BlockSpec(memory_space=pl.ANY),
            pl.BlockSpec(memory_space=pltpu.SMEM),
        ],
        out_specs=pl.BlockSpec(memory_space=pl.ANY),
        scratch_shapes=[
            pltpu.VMEM((mine * m, units * m), jnp.bfloat16),
            dma((mine,)),
            pltpu.VMEM((2 * units, m, width), jnp.bfloat16),
            pltpu.VMEM((units, m, 128), jnp.float32),
            pltpu.VMEM((units, 8, m), jnp.float32),
            pltpu.VMEM((units, units, m, m), jnp.float32),
            pltpu.VMEM((lags - 1, mine, units, m, m), jnp.float32),
            pltpu.VMEM((mine, units, m, m), jnp.bfloat16),
            pltpu.VMEM((mine, units, m, m), jnp.bfloat16),
            dma,
            dma((2, units, SUB)),
            dma((units, SUB)),
            dma((bits, units, SUB)),
            dma((units, SUB)),
            dma((units, units)),
            dma((lags - 1, mine, units)),
            dma((mine, units)),
            dma((mine, units)),
        ],
        compiler_params=pltpu.CompilerParams(
            collective_id=0, has_side_effects=True, vmem_limit_bytes=60 * 2**20
        ),
    )(trajectories.reshape(split, m, width), pair_live)


def solution(mesh):
    size = mesh.shape
    return jax.shard_map(
        functools.partial(on_device, size["row"], size["col"], size["lag"]),
        mesh=mesh,
        in_specs=(P(("row", "col"), "lag"), P()),
        out_specs=P(("row", "lag"), "col"),
        check_vma=False,
    )
```
